32 devices in a mesh: pa: 8 (over z, x), gz: 4 (over y, core).
Axes of the slice: x: 2, y: 2, z: 4, core: 2. Of those that a mesh axis runs over, the one named last changes fastest.
Arguments:
- source: float32 [32, 768, 768], P('gz', 'pa'), may hold values from -24 to 24
- cell_width: float32 [32], P('gz'), may hold values from 0.5 to 2
Outputs:
- potential: float32 [32, 768, 768], P('gz', 'pa')
The draws below stay inside these ranges and needn't reach their ends.
All inputs are finite; a program needn't handle non-finite values.
Results may differ from the reference program's by a relative error of at most 0.00085.
Values sent between devices are 32-bit elements; how exact they have to be, the bound alone decides.
A program may use at most 64 MiB of HBM per device.

```python
import math
import jax
import jax.numpy as jnp
from jax import lax

NX = 768
NY = 768
NZ = 32


def laplace_field(field):
    mirrored = jnp.concatenate([field[:, :, :1], field, field[:, :, -1:]], 2)
    across = 2.0 * field - mirrored[:, :, :-2] - mirrored[:, :, 2:]
    padded_rows = jnp.pad(field, ((0, 0), (1, 1), (0, 0)))
    columns = 2.0 * field - padded_rows[:, :-2, :] - padded_rows[:, 2:, :]
    padded_depth = jnp.pad(field, ((1, 1), (0, 0), (0, 0)))
    along_depth = 2.0 * field - padded_depth[:-2] - padded_depth[2:]
    return across + columns + along_depth


def draw_source(key, part):
    rough = jnp.clip(jax.random.normal(key, (NZ, NY, NX), jnp.float32), -4.0, 4.0)
    return 0.5 * laplace_field(rough)


def shard_levels(stream_key, shape, shards, smallest, top_value):
    gain, own = 1.0, jax.random.fold_in(stream_key, 6)
    for dim, shards_of in shards:
        heights = jnp.exp(jax.random.uniform(jax.random.fold_in(own, dim), (shards_of,), jnp.float32, smallest / len(shards), top_value / len(shards)))
        gain = gain * jnp.repeat(heights, shape[dim] // shards_of).reshape([-1 if axis == dim else 1 for axis in range(len(shape))])
    return gain


def setup_inputs(seed: int = 0) -> dict:
    splits = jax.random.split(jax.random.key(seed), 3)
    return {
        "source": draw_source(jax.random.fold_in(splits[2], 71), 0),
        "cell_width": jnp.clip(jnp.exp(math.log(2.0) - 1.3862944 * jax.random.uniform(splits[1], (NZ,), jnp.float32) ** shard_levels(splits[1], (NZ,), ((0, 4),), -0.2, 0.2)), 0.5, 2.0),
    }


HIGHEST = lax.Precision.HIGHEST

def cosine_table(width):
    counter = jnp.arange(width, dtype=jnp.int32)
    phases = counter[:, None] * (2 * counter[None, :] + 1) % (4 * width)
    angles = phases.astype(jnp.float32) * (math.pi / (2 * width))
    weights = jnp.where(counter == 0, math.sqrt(1.0 / width), math.sqrt(2.0 / width)).astype(jnp.float32)
    return weights[:, None] * jnp.cos(angles)

def sine_table(width):
    counter = jnp.arange(1, width + 1, dtype=jnp.int32)
    phases = counter[:, None] * counter[None, :] % (2 * (width + 1))
    angles = phases.astype(jnp.float32) * (math.pi / (width + 1))
    return math.sqrt(2.0 / (width + 1)) * jnp.sin(angles)

def eigen_first(offset, count, width):
    wavenumber = (offset + jnp.arange(count, dtype=jnp.int32)).astype(jnp.float32)
    return 4.0 * jnp.square(jnp.sin(wavenumber * (math.pi / (2 * width))))

def eigen_second(width):
    wavenumber = jnp.arange(1, width + 1, dtype=jnp.int32).astype(jnp.float32)
    return 4.0 * jnp.square(jnp.sin(wavenumber * (math.pi / (2 * (width + 1)))))

def reference(source, cell_width):
    cos_table = cosine_table(NX)
    sin_table = sine_table(NY)
    padded = jnp.pad(cell_width, 1)
    upper_coef = 2.0 / (padded[1:-1] + padded[2:])
    lower_coef = 2.0 / (padded[:-2] + padded[1:-1])
    along_x = jnp.einsum('zyi,ki->zky', source, cos_table, precision=HIGHEST)
    spectral = jnp.einsum('zkj,lj->zkl', along_x, sin_table, precision=HIGHEST)
    eigen_sum = eigen_first(0, NX, NX)[:, None] + eigen_second(NY)[None, :]

    def eliminate(previous, entries):
        below_coef, above_coef, width_cell, forcing = entries
        diagonal = below_coef + above_coef + width_cell * eigen_sum
        divisor = diagonal + below_coef * previous[0]
        ratio_now = -above_coef / divisor
        value_now = (width_cell * forcing + below_coef * previous[1]) / divisor
        return ((ratio_now, value_now), (ratio_now, value_now))
    zero_plane = jnp.zeros((NX, NY), jnp.float32)
    _, (ratios, values) = lax.scan(eliminate, (zero_plane, zero_plane), (lower_coef, upper_coef, cell_width, spectral))

    def substitute(following, entries):
        current = entries[1] - entries[0] * following
        return (current, current)
    _, solved = lax.scan(substitute, zero_plane, (ratios, values), reverse=True)
    along_y = jnp.einsum('zkl,lj->zkj', solved, sin_table, precision=HIGHEST)
    return jnp.einsum('zky,ki->zyi', along_y, cos_table, precision=HIGHEST)
```

```python
import jax
import jax.numpy as jnp
import numpy as np
from jax import lax
from jax.experimental import pallas as pl
from jax.experimental.pallas import tpu as pltpu
from jax.sharding import PartitionSpec as P

HIGH = lax.Precision.HIGH


def summed_angles(width, coarse, fine, sine):
    f32 = lambda x: jnp.asarray(x.astype(np.float32))
    ca, sa = f32(np.cos(coarse))[:, None, :], f32(np.sin(coarse))[:, None, :]
    cb, sb = f32(np.cos(fine))[None, :, :], f32(np.sin(fine))[None, :, :]
    table = sa * cb + ca * sb if sine else ca * cb - sa * sb
    return table.reshape(width, width)


def split_steps(width):
    step = next(b for b in (32, 16, 8, 1) if width % b == 0)
    return np.arange(0, width, step, dtype=np.int64)[:, None], np.arange(step, dtype=np.int64)[:, None]


def cosine_table(width):
    odd = 2 * np.arange(width, dtype=np.int64)[None, :] + 1
    a, b = (k * odd % (4 * width) * (np.pi / (2 * width)) for k in split_steps(width))
    first = jnp.arange(width)[:, None] == 0
    weights = jnp.where(first, np.sqrt(1.0 / width), np.sqrt(2.0 / width)).astype(jnp.float32)
    return weights * summed_angles(width, a, b, False)


def sine_table(width):
    j = np.arange(1, width + 1, dtype=np.int64)[None, :]
    coarse, fine = split_steps(width)
    a, b = (l * j % (2 * (width + 1)) * (np.pi / (width + 1)) for l in (coarse, fine + 1))
    return np.float32(np.sqrt(2.0 / (width + 1))) * summed_angles(width, a, b, True)


def eigen_first(offset, count, width):
    values = 4.0 * np.sin(np.arange(width) * (np.pi / (2 * width))) ** 2
    return lax.dynamic_slice_in_dim(jnp.asarray(values, jnp.float32), offset, count)[:, None]


def eigen_second(width):
    values = 4.0 * np.sin(np.arange(1, width + 1) * (np.pi / (2 * (width + 1)))) ** 2
    return jnp.asarray(values, jnp.float32)[None, :]


def tiles(rows, width, body):
    lanes = 256 if width % 256 == 0 else width

    if rows % 8:
        for c in range(0, width, lanes):
            body(slice(0, rows), pl.ds(c, lanes))
        return

    def step(r, carry):
        row = pl.ds(pl.multiple_of(r * 8, 8), 8)
        for c in range(0, width, lanes):
            body(row, pl.ds(c, lanes))
        return carry

    lax.fori_loop(0, rows // 8, step, 0)


def ends_kernel(coef, ex, ey, spectral, ends):
    depth, rows, width = spectral.shape

    def body(row, col):
        eigen = ex[row, :] + ey[:, col]
        diag = [coef[0, z] + coef[1, z] + coef[2, z] * eigen for z in range(depth)]
        force = [coef[2, z] * spectral[z, row, col] for z in range(depth)]
        inverse = 1.0 / diag[0]
        value = force[0] * inverse
        other = 1.0 / diag[depth - 1]
        front = force[depth - 1] * other
        for z in range(1, depth):
            inverse = 1.0 / (diag[z] - (coef[0, z] * coef[1, z - 1]) * inverse)
            value = (force[z] + coef[0, z] * value) * inverse
            y = depth - 1 - z
            other = 1.0 / (diag[y] - (coef[1, y] * coef[0, y + 1]) * other)
            front = (force[y] + coef[1, y] * front) * other
        ends[0, row, col] = front
        ends[1, row, col] = value

    tiles(rows, width, body)


def reduced_kernel(coef, ex, ey, ends, sides):
    blocks = ends.shape[0] // 2
    rows, width = ends.shape[1:]
    depth = coef.shape[1] // blocks

    def body(row, col):
        eigen = ex[row, :] + ey[:, col]
        p = jnp.zeros_like(eigen)
        q = jnp.zeros_like(eigen)
        saved = []
        for b in range(blocks):
            s = b * depth
            diag = [coef[0, s + z] + coef[1, s + z] + coef[2, s + z] * eigen for z in range(depth)]
            inverse = 1.0 / diag[0]
            v1 = coef[0, s] * inverse
            other = 1.0 / diag[depth - 1]
            w0 = coef[1, s + depth - 1] * other
            for z in range(1, depth):
                inverse = 1.0 / (diag[z] - (coef[0, s + z] * coef[1, s + z - 1]) * inverse)
                v1 = v1 * (coef[0, s + z] * inverse)
                y = depth - 1 - z
                other = 1.0 / (diag[y] - (coef[1, s + y] * coef[0, s + y + 1]) * other)
                w0 = w0 * (coef[1, s + y] * other)
            w1 = coef[1, s + depth - 1] * inverse
            v0 = coef[0, s] * other
            scale = 1.0 / (1.0 - v0 * q)
            a = (ends[2 * b, row, col] + v0 * p) * scale
            c = w0 * scale
            p, q = ends[2 * b + 1, row, col] + v1 * (p + q * a), v1 * q * c + w1
            saved.append((a, c, p, q))
        head = jnp.zeros_like(eigen)
        for b in reversed(range(blocks)):
            a, c, p, q = saved[b]
            sides[2 * b + 1, row, col] = head
            if b + 1 < blocks:
                sides[2 * b + 2, row, col] = p + q * head
            head = a + c * head
        sides[0, row, col] = jnp.zeros_like(eigen)

    tiles(rows, width, body)


def final_kernel(coef, ex, ey, spectral, sides, solved):
    depth, rows, width = spectral.shape

    def body(row, col):
        eigen = ex[row, :] + ey[:, col]
        ratios, values = [], []
        for z in range(depth):
            diag = coef[0, z] + coef[1, z] + coef[2, z] * eigen
            force = coef[2, z] * spectral[z, row, col]
            if z == 0:
                force = force + coef[0, z] * sides[0, row, col]
            else:
                diag = diag - coef[0, z] * ratios[-1]
                force = force + coef[0, z] * values[-1]
            if z == depth - 1:
                force = force + coef[1, z] * sides[1, row, col]
            inverse = 1.0 / diag
            ratios.append(coef[1, z] * inverse)
            values.append(force * inverse)
        x = values[-1]
        solved[depth - 1, row, col] = x
        for z in reversed(range(depth - 1)):
            x = values[z] + ratios[z] * x
            solved[z, row, col] = x

    tiles(rows, width, body)


def solve_call(kernel, leads, lead_out, coef, ex, ey, *planes):
    rows, width = planes[0].shape[1:]
    block = next((b for b in (32, 24, 16, 8) if rows % b == 0), rows)
    spec = lambda lead: pl.BlockSpec((lead, block, width), lambda i: (0, i, 0))
    return pl.pallas_call(
        kernel,
        grid=(rows // block,),
        in_specs=[
            pl.BlockSpec(memory_space=pltpu.SMEM),
            pl.BlockSpec((block, 1), lambda i: (i, 0)),
            pl.BlockSpec((1, width), lambda i: (0, 0)),
        ]
        + [spec(lead) for lead in leads],
        out_specs=spec(lead_out),
        out_shape=jax.ShapeDtypeStruct((lead_out, rows, width), jnp.float32),
    )(coef, ex, ey, *planes)


def on_device(source, cell_width):
    depth, rows_local, width_x = source.shape
    blocks = lax.axis_size("gz")
    width_y = rows_local * lax.axis_size("pa")
    cos_table = cosine_table(width_x)
    sin_table = sine_table(width_y)
    block = lax.axis_index("gz")
    widths = lax.all_gather(cell_width, "gz", tiled=True)
    padded = jnp.pad(widths, 1)
    coef = jnp.stack(
        [2.0 / (padded[:-2] + widths), 2.0 / (widths + padded[2:]), widths]
    )
    own = lax.dynamic_slice_in_dim(coef, block * depth, depth, axis=1)
    along_x = jnp.einsum("zyi,ki->zky", source, cos_table, precision=HIGH)
    spectral = jnp.einsum(
        "zkj,lj->zkl",
        lax.all_to_all(along_x, "pa", split_axis=1, concat_axis=2, tiled=True),
        sin_table,
        precision=HIGH,
    )
    kx = spectral.shape[1]
    first = lax.axis_index("pa") * kx
    part = kx // blocks
    ex = eigen_first(first, kx, width_x)
    ex_part = eigen_first(first + block * part, part, width_x)
    ey = eigen_second(width_y)
    ends = solve_call(ends_kernel, (depth,), 2, own, ex, ey, spectral)
    ends = lax.all_to_all(ends, "gz", split_axis=1, concat_axis=0, tiled=True)
    sides = solve_call(reduced_kernel, (2 * blocks,), 2 * blocks, coef, ex_part, ey, ends)
    sides = lax.all_to_all(sides, "gz", split_axis=0, concat_axis=1, tiled=True)
    solved = solve_call(final_kernel, (depth, 2), depth, own, ex, ey, spectral, sides)
    along_y = jnp.einsum("zkl,lj->zkj", solved, sin_table, precision=HIGH)
    return jnp.einsum(
        "zky,ki->zyi",
        lax.all_to_all(along_y, "pa", split_axis=2, concat_axis=1, tiled=True),
        cos_table,
        precision=HIGH,
    )


def solution(mesh):
    in_specs = (P("gz", "pa", None), P("gz"))
    out_specs = P("gz", "pa", None)
    return jax.shard_map(
        on_device, mesh=mesh, in_specs=in_specs, out_specs=out_specs, check_vma=False
    )
```
